32 devices in a mesh: group: 4 (over y, x), passage: 8 (over z, core).
Axes of the slice: x: 2, y: 2, z: 4, core: 2. Of those that a mesh axis runs over, the one named last changes fastest.
Arguments:
- decoder_states: bfloat16 [4, 256, 4096], P('group', None, 'passage'), may hold values from -6 to 6
- w_query: bfloat16 [4096, 2048], P('passage'), may hold values from -0.09375 to 0.09375
- passage_keys: bfloat16 [4, 2048, 2048], P('group', 'passage'), may hold values from -256 to 256
- passage_values: bfloat16 [4, 2048, 2048], P('group', 'passage'), may hold values from -6 to 6
- grad_context: bfloat16 [4, 256, 2048], P('group', None, 'passage'), may hold values from -384 to 384
- key_len: int32 [4, 16], P('group', 'passage'), may hold values from 32 to 128, as said below
- tgt_len: int32 [4], P('group'), may hold values from 64 to 256, as said below
Outputs:
- grad_states: bfloat16 [4, 256, 4096], P('group', None, 'passage')
- grad_query_weight: float32 [4096, 2048], P('passage', 'group')
- grad_keys: bfloat16 [4, 2048, 2048], P('group', 'passage')
- grad_values: bfloat16 [4, 2048, 2048], P('group', 'passage')
The draws below stay inside these ranges and needn't reach their ends.
Inputs may be any that keep to these rules, and one draw needn't show every extreme that they name: `key_len`: every question has at least one passage with all 128 slots used. `tgt_len`: some question uses all 256 target positions.
All inputs are finite; a program needn't handle non-finite values.
Results may differ from the reference program's by a relative error of at most 0.0065.
The reference program's roundings to bfloat16 on the way (of `queries`, `cotangent`, `dscore` and `query_grad`) count: a program that leaves them out, or rounds other values in their place, can miss the bound.
Values may be sent and summed in bfloat16 or wider, within the bound.
No kernel may reach another device: no remote copies, remote signals or barrier semaphores. Data moves between devices by JAX's collectives and lax.ppermute only.
A program may use at most 64 MiB of HBM per device.

```python
import jax
import jax.numpy as jnp
from jax import lax

D = 4096
DH = 64
TGT = 256
PLEN = 128
HD = 2048
NQ = 4
PASSAGES = 16
KEYS = 2048


def shared_inputs(key):
    state_key = jax.random.fold_in(key, 101)
    weight_key = jax.random.fold_in(key, 102)
    states = jnp.clip(jax.random.normal(state_key, (NQ, TGT, D), jnp.float32), -6.0, 6.0)
    weights = jnp.clip(jax.random.normal(weight_key, (D, HD), jnp.float32), -6.0, 6.0) * D ** (-0.5)
    return (states.astype(jnp.bfloat16), weights.astype(jnp.bfloat16))


def draw_decoder_states(key, part):
    return shared_inputs(key)[0]


def draw_w_query(key, part):
    return shared_inputs(key)[1]


def draw_key_len(key, part):
    length_key = jax.random.fold_in(key, 103)
    lengths = jax.random.randint(length_key, (NQ, PASSAGES), PLEN // 4, PLEN + 1)
    full_one = jax.random.randint(jax.random.fold_in(length_key, 1), (NQ, 1), 0, PASSAGES)
    lengths = jnp.where(jnp.arange(PASSAGES)[None, :] == full_one, PLEN, lengths)
    return lengths.astype(jnp.int32)


def draw_tgt_len(key, part):
    length_key = jax.random.fold_in(key, 106)
    lengths = jax.random.randint(length_key, (NQ,), TGT // 4, TGT + 1)
    full_one = jax.random.randint(jax.random.fold_in(length_key, 1), (), 0, NQ)
    lengths = jnp.where(jnp.arange(NQ) == full_one, TGT, lengths)
    return lengths.astype(jnp.int32)


def draw_passage_keys(key, part):
    base_key = jax.random.fold_in(key, 104)
    base = jnp.clip(jax.random.normal(base_key, (NQ, KEYS, HD), jnp.float32), -4.0, 4.0)
    return base.astype(jnp.bfloat16)


def levels(key, dims, cuts, smallest, largest):
    factor_of = 1.0
    for dim, parts in cuts:
        steps = jax.random.uniform(jax.random.fold_in(jax.random.fold_in(key, 6), dim), (parts,), jnp.float32, smallest / len(cuts), largest / len(cuts))
        factor_of = factor_of * jnp.repeat(jnp.exp(steps), dims[dim] // parts).reshape((-1,) + (1,) * (len(dims) - 1 - dim))
    return factor_of


def noise(own_key, extent, spread, limit, cuts=(), kind=jnp.bfloat16):
    drawn = spread * jax.random.normal(own_key, extent, jnp.float32)
    if cuts:
        drawn = drawn * levels(own_key, extent, cuts, -0.22, 0.18)
    return jnp.clip(drawn, -limit, limit).astype(kind)


def setup_inputs(seed: int = 0) -> dict:
    splits = jax.random.split(jax.random.key(seed), 8)
    decoder_states = draw_decoder_states(jax.random.fold_in(splits[7], 71), 0)
    w_query = draw_w_query(jax.random.fold_in(splits[7], 71), 0)
    passage_keys = draw_passage_keys(jax.random.fold_in(splits[7], 71), 0)
    passage_values = noise(splits[3], (NQ, KEYS, HD), 1.0, 6.0, ((0, 4), (1, 8)))
    grad_context = noise(splits[4], (NQ, TGT, HD), 64.0, 384.0, ((0, 4), (2, 8)))
    key_len = draw_key_len(jax.random.fold_in(splits[7], 71), 0)
    tgt_len = draw_tgt_len(jax.random.fold_in(splits[7], 71), 0)
    return dict(decoder_states=decoder_states, w_query=w_query, passage_keys=passage_keys, passage_values=passage_values, grad_context=grad_context, key_len=key_len, tgt_len=tgt_len)


def question_grads(inputs):
    queries, keys_here, values_here, cotangent, key_valid = inputs
    heads = HD // DH
    score_scale = DH ** -0.5
    query_heads = queries.astype(jnp.float32).reshape(TGT, heads, DH)
    key_heads = keys_here.astype(jnp.float32).reshape(KEYS, heads, DH)
    value_heads = values_here.astype(jnp.float32).reshape(KEYS, heads, DH)
    cot_heads = cotangent.astype(jnp.float32).reshape(TGT, heads, DH)
    scores = jnp.einsum('the,khe->htk', query_heads, key_heads) * score_scale
    scores = jnp.where(key_valid[None, None, :], scores, -jnp.inf)
    peak = jnp.max(scores, axis=-1, keepdims=True)
    expo = jnp.exp(scores - peak)
    total = jnp.sum(expo, axis=-1, keepdims=True)
    probs = expo / total
    dprob = jnp.einsum('the,khe->htk', cot_heads, value_heads)
    row_dot = jnp.sum(probs * dprob, axis=-1, keepdims=True)
    probs_low = lax.optimization_barrier(probs.astype(jnp.bfloat16)).astype(jnp.float32)
    dscore = lax.optimization_barrier((probs * (dprob - row_dot)).astype(jnp.bfloat16)).astype(jnp.float32)
    grad_values = jnp.einsum('htk,the->khe', probs_low, cot_heads).reshape(KEYS, HD).astype(jnp.bfloat16)
    grad_keys = (jnp.einsum('htk,the->khe', dscore, query_heads) * score_scale).reshape(KEYS, HD).astype(jnp.bfloat16)
    query_grad = (jnp.einsum('htk,khe->the', dscore, key_heads) * score_scale).reshape(TGT, HD)
    return query_grad, grad_keys, grad_values


def reference(decoder_states, w_query, passage_keys, passage_values, grad_context, key_len, tgt_len):
    states = decoder_states.astype(jnp.float32)
    weights = w_query.astype(jnp.float32)
    queries = jnp.einsum('ntd,de->nte', states, weights).astype(jnp.bfloat16)
    positions = jnp.arange(KEYS)
    key_lengths = key_len[:, positions // PLEN]
    key_valid = (positions % PLEN)[None, :] < key_lengths
    row_valid = jnp.arange(TGT)[None, :] < tgt_len[:, None]
    cotangent = jnp.where(row_valid[:, :, None], grad_context, jnp.zeros((), grad_context.dtype))
    query_grad, grad_keys, grad_values = lax.map(question_grads, (queries, passage_keys, passage_values, cotangent, key_valid))
    query_low = lax.optimization_barrier(query_grad.astype(jnp.bfloat16)).astype(jnp.float32)
    grad_states = jnp.einsum('nte,de->ntd', query_low, weights).astype(jnp.bfloat16)
    grad_query_weight = jnp.einsum('ntd,nte->de', states, query_low) / decoder_states.shape[0]
    return grad_states, grad_query_weight, grad_keys, grad_values
```

```python
import functools

import jax
import jax.numpy as jnp
from jax import lax
from jax.experimental import pallas as pl
from jax.experimental.pallas import tpu as pltpu
from jax.sharding import PartitionSpec as P

DH = 64
PLEN = 128
LANES = 128
HPAIR = LANES // DH
F32 = jnp.float32
BF16 = jnp.bfloat16
NT = (((1,), (1,)), ((), ()))


def merged(part, axis, combine):
    gathered = jax.tree.map(lambda a: lax.all_gather(a, axis), part)

    def take(source):
        return jax.tree.map(lambda a: lax.dynamic_index_in_dim(a, source, 0, False), gathered)

    return lax.fori_loop(
        1, lax.axis_size(axis), lambda source, state: combine(state, take(source)), take(0)
    )


def combine_stats(earlier, later):
    peak_a, total_a, weighted_a = earlier
    peak_b, total_b, weighted_b = later
    peak = jnp.maximum(peak_a, peak_b)
    factor_a = jnp.exp(peak_a - peak)
    factor_b = jnp.exp(peak_b - peak)
    return (
        peak,
        total_a * factor_a + total_b * factor_b,
        weighted_a * factor_a + weighted_b * factor_b,
    )


def on_device_general(
    decoder_states, w_query, passage_keys, passage_values, grad_context, key_len, tgt_len
):
    score_scale = DH ** (-0.5)
    states = decoder_states[0]
    target_rows = states.shape[0]
    query_part = jnp.dot(states, w_query, preferred_element_type=F32)
    queries = lax.psum(query_part, "passage").astype(BF16)
    cotangent = lax.all_gather(grad_context[0], "passage", axis=1, tiled=True)
    row_valid = jnp.arange(target_rows) < tgt_len[0]
    cotangent = jnp.where(row_valid[:, None], cotangent, jnp.zeros((), BF16))
    keys_here = passage_keys[0]
    values_here = passage_values[0]
    key_count, width = keys_here.shape
    heads = width // DH
    positions = jnp.arange(key_count)
    owner = positions // PLEN
    passage_ids = jnp.arange(key_len.shape[1])
    key_lengths = jnp.sum(
        jnp.where(owner[:, None] == passage_ids[None, :], key_len[0][None, :], 0), axis=1
    )
    key_valid = positions % PLEN < key_lengths
    query_heads = queries.reshape(target_rows, heads, DH)
    key_heads = keys_here.reshape(key_count, heads, DH)
    value_heads = values_here.reshape(key_count, heads, DH)
    cot_heads = cotangent.reshape(target_rows, heads, DH)
    scores = (
        jnp.einsum("the,khe->htk", query_heads, key_heads, preferred_element_type=F32)
        * score_scale
    )
    scores = jnp.where(key_valid[None, None, :], scores, -jnp.inf)
    dprob = jnp.einsum("the,khe->htk", cot_heads, value_heads, preferred_element_type=F32)
    local_peak = jnp.max(scores, axis=2)
    local_expo = jnp.exp(scores - local_peak[:, :, None])
    peak, total, weighted = merged(
        (local_peak, jnp.sum(local_expo, axis=2), jnp.sum(local_expo * dprob, axis=2)),
        "passage",
        combine_stats,
    )
    expo = local_expo * jnp.exp(local_peak - peak)[:, :, None]
    probs = expo / total[:, :, None]
    row_dot = weighted / total
    probs_low = probs.astype(BF16)
    dscore = (probs * (dprob - row_dot[:, :, None])).astype(BF16)
    grad_values = jnp.einsum("htk,the->khe", probs_low, cot_heads, preferred_element_type=F32)
    grad_values = grad_values.reshape(key_count, width).astype(BF16)
    grad_keys = (
        jnp.einsum("htk,the->khe", dscore, query_heads, preferred_element_type=F32) * score_scale
    )
    grad_keys = grad_keys.reshape(key_count, width).astype(BF16)
    query_grad_part = (
        jnp.einsum("htk,khe->the", dscore, key_heads, preferred_element_type=F32) * score_scale
    )
    query_grad_part = query_grad_part.reshape(target_rows, width)
    query_grad = lax.psum(query_grad_part, "passage").astype(BF16)
    grad_states = lax.dot_general(query_grad, w_query, NT, preferred_element_type=F32)
    grad_states = grad_states.astype(BF16)
    weight_term = lax.dot_general(
        states, query_grad, (((0,), (0,)), ((), ())), preferred_element_type=F32
    )
    weight_term = weight_term / lax.axis_size("group")
    grad_query_weight = lax.psum_scatter(weight_term, "group", scatter_dimension=1, tiled=True)
    return (grad_states[None], grad_query_weight, grad_keys[None], grad_values[None])


def column(who, r, other):
    node, core = who[0] // 2, who[0] % 2
    return 2 * (node ^ r) + (1 - core if other else core)


def pack_call(who, keys, values, blocks, width):
    rows = keys.shape[0]

    def kernel(who_ref, k_ref, v_ref, o_ref):
        o_ref[0, 0] = k_ref[...]
        o_ref[1, 0] = v_ref[...]

    source = pl.BlockSpec((rows, width), lambda r, who_ref: (0, column(who_ref, r, True)))
    return pl.pallas_call(
        kernel,
        out_shape=jax.ShapeDtypeStruct((2, blocks, rows, width), BF16),
        grid_spec=pltpu.PrefetchScalarGridSpec(
            num_scalar_prefetch=1,
            grid=(blocks,),
            in_specs=[source, source],
            out_specs=pl.BlockSpec((2, 1, rows, width), lambda r, who_ref: (0, r, 0, 0)),
        ),
        name="pack",
    )(who, keys, values)


def project_call(who, states, weights, picks, width, addend=None):
    first, step, count = picks
    rows, depth = states.shape
    other = addend is None

    def kernel(who_ref, s_ref, w_ref, *rest):
        part = jnp.dot(s_ref[...], w_ref[...], preferred_element_type=F32)
        if other:
            rest[0][0] = part
            return
        part = part + rest[0][0]
        for i in range(count):

            @pl.when(pl.program_id(0) == i)
            def _(i=i):
                rest[1 + i][...] = part

    in_specs = [
        pl.BlockSpec((rows, depth), lambda i, who_ref: (0, 0)),
        pl.BlockSpec((depth, width), lambda i, who_ref: (0, column(who_ref, first + step * i, other))),
    ]
    stacked = pl.BlockSpec((1, rows, width), lambda i, who_ref: (i, 0, 0))
    args = [who, states, weights]
    if other:
        out_shape = jax.ShapeDtypeStruct((count, rows, width), F32)
        out_specs = stacked
    else:
        in_specs.append(stacked)
        args.append(addend)
        out_shape = [jax.ShapeDtypeStruct((rows, width), F32)] * count
        out_specs = [pl.BlockSpec((rows, width), lambda i, who_ref: (0, 0))] * count
    return pl.pallas_call(
        kernel,
        out_shape=out_shape,
        grid_spec=pltpu.PrefetchScalarGridSpec(
            num_scalar_prefetch=1, grid=(count,), in_specs=in_specs, out_specs=out_specs
        ),
        name="project",
    )(*args)


def lane_half(shape, e):
    return lax.broadcasted_iota(jnp.int32, shape, 1) // DH == e


def key_bias(lens_ref, rows):
    slot = lax.broadcasted_iota(jnp.int32, (rows, 1), 0)
    limit = jnp.zeros((rows, 1), jnp.int32)
    for i in range(rows // PLEN):
        limit = jnp.where(slot // PLEN == i, lens_ref[i], limit)
    return jnp.where(slot % PLEN < limit, 0.0, -jnp.inf).astype(F32)


def masked_cot(tgt_ref, cot):
    row = lax.broadcasted_iota(jnp.int32, cot.shape, 0)
    return jnp.where(row < tgt_ref[0], cot, jnp.zeros((), cot.dtype))


SEGS = 2


def attend_in(r, rows, keys, width):
    pairs = width // LANES

    def own(i, who_ref, *_):
        return (0, column(who_ref, r, False) * pairs + i)

    def pair(i, *_):
        return (0, i)

    return [
        pl.BlockSpec((rows, LANES), pair),
        pl.BlockSpec((rows, LANES), pair),
        pl.BlockSpec((keys, LANES), own),
        pl.BlockSpec((keys, LANES), own),
        pl.BlockSpec((1, 1, keys, LANES), lambda i, *_: (0, r, 0, i)),
        pl.BlockSpec((1, 1, keys, LANES), lambda i, *_: (1, r, 0, i)),
    ]


def stats_call(scalars, q, cot, keys, values, from_mate, r, stats):
    rows, width = q.shape
    slots = keys.shape[0]
    pairs = width // LANES
    heads = width // DH
    blocks = from_mate.shape[1]
    scale = DH ** (-0.5)

    def kernel(who_ref, len_ref, mate_ref, tgt_ref, q_ref, c_ref, k_ref, v_ref, km_ref, vm_ref, *rest):
        o_ref = rest[-1]
        bias = (key_bias(len_ref, slots), key_bias(mate_ref, slots))
        k = (k_ref[...], km_ref[0, 0])
        v = (v_ref[...], vm_ref[0, 0])
        qs = q_ref[...] * jnp.asarray(scale, BF16)
        ct = masked_cot(tgt_ref, c_ref[...])
        out = []
        for e in range(HPAIR):
            lanes = lane_half((rows, LANES), e)
            qm = jnp.where(lanes, qs, jnp.zeros((), BF16))
            cm = jnp.where(lanes, ct, jnp.zeros((), BF16))
            s = [lax.dot_general(k[i], qm, NT, preferred_element_type=F32) + bias[i] for i in range(SEGS)]
            d = [lax.dot_general(v[i], cm, NT, preferred_element_type=F32) for i in range(SEGS)]
            peak = jnp.maximum(*[jnp.max(x, axis=0, keepdims=True) for x in s])
            x = [jnp.exp(y - peak) for y in s]
            total = sum(jnp.sum(y, axis=0, keepdims=True) for y in x)
            weighted = sum(jnp.sum(y * w, axis=0, keepdims=True) for y, w in zip(x, d, strict=True))
            out.append((peak, total, weighted))
        for pair in range(pairs):

            @pl.when(pl.program_id(0) == pair)
            def _(pair=pair):
                for kind in range(3):
                    for e in range(HPAIR):
                        row = kind * heads + pair * HPAIR + e
                        o_ref[0, row : row + 1, :] = out[e][kind]

    args = [*scalars, q, cot, keys, values, from_mate, from_mate]
    in_specs = attend_in(r, rows, slots, width)
    aliases = {}
    if stats is not None:
        aliases = {len(args): 0}
        args.append(stats)
        in_specs.append(pl.BlockSpec(memory_space=pl.ANY))
    return pl.pallas_call(
        kernel,
        out_shape=jax.ShapeDtypeStruct((blocks, 3 * heads, rows), F32),
        grid_spec=pltpu.PrefetchScalarGridSpec(
            num_scalar_prefetch=len(scalars),
            grid=(pairs,),
            in_specs=in_specs,
            out_specs=pl.BlockSpec((1, 3 * heads, rows), lambda i, *_: (r, 0, 0)),
        ),
        input_output_aliases=aliases,
        name="stats",
    )(*args)


def grads_call(scalars, q, cot, keys, values, from_mate, stats, r, chain):
    rows, width = q.shape
    slots, full = keys.shape
    pairs = width // LANES
    heads = width // DH
    blocks = from_mate.shape[1]
    scale = DH ** (-0.5)

    def kernel(who_ref, len_ref, mate_ref, tgt_ref, q_ref, c_ref, k_ref, v_ref, km_ref, vm_ref, st_ref, *rest):
        g_ref, gk_ref, gv_ref, gm_ref = rest[-4:]
        bias = (key_bias(len_ref, slots), key_bias(mate_ref, slots))
        k = (k_ref[...], km_ref[0, 0])
        v = (v_ref[...], vm_ref[0, 0])
        qs = q_ref[...] * jnp.asarray(scale, BF16)
        ct = masked_cot(tgt_ref, c_ref[...])
        grad_k = [None] * SEGS
        grad_v = [None] * SEGS
        grad_q = []
        turned = [x.T for x in k]
        for e in range(HPAIR):
            lanes = lane_half((rows, LANES), e)
            qm = jnp.where(lanes, qs, jnp.zeros((), BF16))
            cm = jnp.where(lanes, ct, jnp.zeros((), BF16))
            row = pl.program_id(0) * HPAIR + e
            peak = st_ref[0, pl.ds(row, 1), :]
            share = st_ref[0, pl.ds(heads + row, 1), :]
            dot = st_ref[0, pl.ds(2 * heads + row, 1), :]
            part = 0.0
            for i in range(SEGS):
                s = lax.dot_general(k[i], qm, NT, preferred_element_type=F32) + bias[i]
                d = lax.dot_general(v[i], cm, NT, preferred_element_type=F32)
                probs = jnp.exp(s - peak) * share
                low = probs.astype(BF16)
                ds = (probs * (d - dot)).astype(BF16)
                gv = jnp.dot(low, cm, preferred_element_type=F32)
                gk = jnp.dot(ds, qm, preferred_element_type=F32)
                grad_v[i] = gv if e == 0 else grad_v[i] + gv
                grad_k[i] = gk if e == 0 else grad_k[i] + gk
                part = part + jnp.dot(turned[i][e * DH : (e + 1) * DH], ds, preferred_element_type=F32)
            grad_q.append(part)
        g_ref[...] = (jnp.concatenate(grad_q, axis=0) * scale).T
        gk_ref[...] = grad_k[0].astype(BF16)
        gv_ref[...] = grad_v[0].astype(BF16)
        gm_ref[0, 0] = grad_k[1].astype(BF16)
        gm_ref[1, 0] = grad_v[1].astype(BF16)

    args = [*scalars, q, cot, keys, values, from_mate, from_mate, stats]
    specs = attend_in(r, rows, slots, width)
    in_specs = [*specs, pl.BlockSpec((1, 3 * heads, rows), lambda i, *_: (r, 0, 0))]
    aliases = {}
    if chain is not None:
        aliases = {len(args) + i: 1 + i for i in range(3)}
        args += chain
        in_specs += [pl.BlockSpec(memory_space=pl.ANY)] * 3
    out = pl.pallas_call(
        kernel,
        out_shape=[
            jax.ShapeDtypeStruct((rows, width), F32),
            jax.ShapeDtypeStruct((slots, full), BF16),
            jax.ShapeDtypeStruct((slots, full), BF16),
            jax.ShapeDtypeStruct((2, blocks, slots, width), BF16),
        ],
        grid_spec=pltpu.PrefetchScalarGridSpec(
            num_scalar_prefetch=len(scalars),
            grid=(pairs,),
            in_specs=in_specs,
            out_specs=[
                specs[0],
                specs[2],
                specs[3],
                pl.BlockSpec((2, 1, slots, LANES), lambda i, *_: (0, r, 0, i)),
            ],
        ),
        input_output_aliases=aliases,
        name="grads",
    )(*args)
    return out[0], list(out[1:])


def merge_call(who, grad_k, grad_v, from_mate):
    slots, full = grad_k.shape
    _, blocks, _, width = from_mate.shape

    def kernel(who_ref, k_in, v_in, m_ref, k_ref, v_ref):
        k_ref[...] = m_ref[0, 0]
        v_ref[...] = m_ref[1, 0]

    target = pl.BlockSpec((slots, width), lambda r, who_ref: (0, column(who_ref, r, True)))
    return pl.pallas_call(
        kernel,
        out_shape=[jax.ShapeDtypeStruct((slots, full), BF16)] * 2,
        grid_spec=pltpu.PrefetchScalarGridSpec(
            num_scalar_prefetch=1,
            grid=(blocks,),
            in_specs=[
                pl.BlockSpec(memory_space=pl.ANY),
                pl.BlockSpec(memory_space=pl.ANY),
                pl.BlockSpec((2, 1, slots, width), lambda r, who_ref: (0, r, 0, 0)),
            ],
            out_specs=[target, target],
        ),
        input_output_aliases={1: 0, 2: 1},
        name="merge",
    )(who, grad_k, grad_v, from_mate)


def states_call(who, mine, mates, weights):
    blocks, rows, width = mine.shape
    depth = weights.shape[0]

    def kernel(who_ref, a_ref, b_ref, wa_ref, wb_ref, o_ref, acc):
        part = lax.dot_general(a_ref[0], wa_ref[...], NT, preferred_element_type=F32)
        part += lax.dot_general(b_ref[0], wb_ref[...], NT, preferred_element_type=F32)
        step = pl.program_id(0)

        @pl.when(step == 0)
        def _():
            acc[...] = part

        @pl.when(step > 0)
        def _():
            acc[...] += part

        @pl.when(step == blocks - 1)
        def _():
            o_ref[...] = acc[...].astype(BF16)

    block = pl.BlockSpec((1, rows, width), lambda r, who_ref: (r, 0, 0))
    return pl.pallas_call(
        kernel,
        out_shape=jax.ShapeDtypeStruct((rows, depth), BF16),
        grid_spec=pltpu.PrefetchScalarGridSpec(
            num_scalar_prefetch=1,
            grid=(blocks,),
            in_specs=[
                block,
                block,
                pl.BlockSpec((depth, width), lambda r, who_ref: (0, column(who_ref, r, False))),
                pl.BlockSpec((depth, width), lambda r, who_ref: (0, column(who_ref, r, True))),
            ],
            out_specs=pl.BlockSpec((rows, depth), lambda r, who_ref: (0, 0)),
            scratch_shapes=[pltpu.VMEM((rows, depth), F32)],
        ),
        name="states",
    )(who, mine, mates, weights, weights)


def weight_call(who, turned, mine, mates):
    depth = turned.shape[0]
    groups, rows, width = mine.shape

    def kernel(who_ref, s_ref, a_ref, b_ref, o_ref):
        for i, ref in enumerate((a_ref, b_ref)):

            @pl.when(pl.program_id(0) == i)
            def _(ref=ref):
                total = 0.0
                for s in range(groups):
                    total += jnp.dot(
                        s_ref[:, s * rows : (s + 1) * rows], ref[s], preferred_element_type=F32
                    )
                o_ref[...] = total / groups

    whole = pl.BlockSpec((groups, rows, width), lambda i, who_ref: (0, 0, 0))
    return pl.pallas_call(
        kernel,
        out_shape=jax.ShapeDtypeStruct((depth, 2 * width), F32),
        grid_spec=pltpu.PrefetchScalarGridSpec(
            num_scalar_prefetch=1,
            grid=(2,),
            in_specs=[
                pl.BlockSpec((depth, groups * rows), lambda i, who_ref: (0, 0)),
                whole,
                whole,
            ],
            out_specs=pl.BlockSpec((depth, width), lambda i, who_ref: (0, (who_ref[0] + i) % 2)),
        ),
        name="weight",
    )(who, turned, mine, mates)


def swap(x, bit):
    count = lax.axis_size("passage")
    return lax.ppermute(x, "passage", [(i, i ^ bit) for i in range(count)])


def group_swap(x, bits):
    count = lax.axis_size("group")
    return lax.ppermute(x, "group", [(i, i ^ bits) for i in range(count)])


def halve(pieces, nodes):
    bit = 1
    while bit < nodes:
        sent = [r for r in range(nodes - 1, -1, -1) if r & bit and r % bit == 0]
        for r in sent:
            pieces[r ^ bit] = pieces[r ^ bit] + swap(pieces[r], 2 * bit)
        bit *= 2
    return pieces[0]


def double(own, nodes):
    held = {0: own}
    bit = nodes // 2
    while bit:
        held.update({r ^ bit: swap(x, 2 * bit) for r, x in list(held.items())})
        bit //= 2
    return [held[r] for r in range(nodes)]


def combine_rows(mine, other, heads):
    peak = jnp.maximum(mine[:, :heads], other[:, :heads])
    mine_by = jnp.exp(mine[:, :heads] - peak)
    other_by = jnp.exp(other[:, :heads] - peak)
    total = mine[:, heads : 2 * heads] * mine_by + other[:, heads : 2 * heads] * other_by
    weighted = mine[:, 2 * heads :] * mine_by + other[:, 2 * heads :] * other_by
    return jnp.concatenate([peak, total, weighted], axis=1)


def on_device(
    decoder_states, w_query, passage_keys, passage_values, grad_context, key_len, tgt_len
):
    nodes = lax.axis_size("passage") // 2
    groups = lax.axis_size("group")
    me = lax.axis_index("passage")
    node = me // 2
    group = lax.axis_index("group")
    who = jnp.full((1,), me, jnp.int32)
    states = decoder_states[0]
    rows = states.shape[0]
    keys, values = passage_keys[0], passage_values[0]
    width = grad_context.shape[2]
    heads = width // DH

    cots = double(grad_context[0], nodes)
    odd = (nodes - 1, -2, nodes // 2)
    even = (nodes - 2, -2, nodes // 2)
    odd_mate = swap(project_call(who, states, w_query, odd, width), 1)
    even_mate = swap(project_call(who, states, w_query, even, width), 1)
    parts = {}
    for picks, mate in ((odd, odd_mate), (even, even_mate)):
        out = project_call(who, states, w_query, picks, width, mate)
        parts.update({picks[0] + picks[1] * i: x for i, x in enumerate(out)})
    own_query = halve(parts, nodes).astype(BF16)
    queries = double(own_query, nodes)

    mate_len = swap(key_len[0], 1)
    from_mate = swap(pack_call(who, keys, values, nodes, width), 1)
    scalars = (who, key_len[0], mate_len, tgt_len)
    questions = [states] + [group_swap(states, s) for s in range(1, groups)]
    turned = jnp.concatenate([x.T for x in questions], axis=1)

    stats = None
    for r in sorted(range(nodes), key=lambda r: (r & 1, r)):
        stats = stats_call(scalars, queries[r], cots[r], keys, values, from_mate, r, stats)
    bit = 1
    while bit < nodes:
        other = swap(stats, 2 * bit)
        other = jnp.stack([other[r ^ bit] for r in range(nodes)])
        stats = combine_rows(stats, other, heads)
        bit *= 2
    total = stats[:, heads : 2 * heads]
    stats = jnp.concatenate([stats[:, :heads], 1.0 / total, stats[:, 2 * heads :] / total], axis=1)

    parts, chain = {}, None
    for r in [*range(nodes - 1, 0, -2), *range(nodes - 2, -1, -2)]:
        parts[r], chain = grads_call(
            scalars, queries[r], cots[r], keys, values, from_mate, stats, r, chain
        )
    grad_k, grad_v = merge_call(who, chain[0], chain[1], swap(chain[2], 1))
    own_grad = halve(parts, nodes).astype(BF16)
    mine = jnp.stack(double(own_grad, nodes))

    def block_of(target):
        return lax.dynamic_index_in_dim(mine, target ^ node, 0, False)

    got = [block_of(group)] + [group_swap(block_of(group ^ s), s) for s in range(1, groups)]
    got = jnp.stack(got)
    grad_states = states_call(who, mine, swap(mine, 1), w_query)
    grad_weight = weight_call(who, turned, got, swap(got, 1))
    return (grad_states[None], grad_weight, grad_k[None], grad_v[None])


def solution(mesh):
    placed = (
        P("group", None, "passage"),
        P("passage", None),
        P("group", "passage", None),
        P("group", "passage", None),
        P("group", None, "passage"),
        P("group", "passage"),
        P("group"),
    )

    def whole(*args):
        groups, count = mesh.shape["group"], mesh.shape["passage"]
        paired = 2 * groups == count and count & (count - 1) == 0
        blocked = args[4].shape[2] % (count * LANES) == 0
        body = on_device if paired and blocked else on_device_general
        return jax.shard_map(
            body,
            mesh=mesh,
            in_specs=placed,
            out_specs=(
                P("group", None, "passage"),
                P("passage", "group"),
                P("group", "passage", None),
                P("group", "passage", None),
            ),
            check_vma=False,
        )(*args)

    return whole
```

```python
import jax
import jax.numpy as jnp
from jax import lax
from jax.experimental import pallas as pl
from jax.experimental.pallas import tpu as pltpu
from jax.sharding import PartitionSpec as P

DH = 64
PLEN = 128
LANES = 128
HPAIR = LANES // DH
F32 = jnp.float32
BF16 = jnp.bfloat16
NT = (((1,), (1,)), ((), ()))


def merged(part, axis, combine):
    gathered = jax.tree.map(lambda a: lax.all_gather(a, axis), part)

    def take(source):
        return jax.tree.map(lambda a: lax.dynamic_index_in_dim(a, source, 0, False), gathered)

    return lax.fori_loop(
        1, lax.axis_size(axis), lambda source, state: combine(state, take(source)), take(0)
    )


def combine_stats(earlier, later):
    peak_a, total_a, weighted_a = earlier
    peak_b, total_b, weighted_b = later
    peak = jnp.maximum(peak_a, peak_b)
    factor_a = jnp.exp(peak_a - peak)
    factor_b = jnp.exp(peak_b - peak)
    return (
        peak,
        total_a * factor_a + total_b * factor_b,
        weighted_a * factor_a + weighted_b * factor_b,
    )


def on_device_general(
    decoder_states, w_query, passage_keys, passage_values, grad_context, key_len, tgt_len
):
    score_scale = DH ** (-0.5)
    states = decoder_states[0]
    target_rows = states.shape[0]
    query_part = jnp.dot(states, w_query, preferred_element_type=F32)
    queries = lax.psum(query_part, "passage").astype(BF16)
    cotangent = lax.all_gather(grad_context[0], "passage", axis=1, tiled=True)
    row_valid = jnp.arange(target_rows) < tgt_len[0]
    cotangent = jnp.where(row_valid[:, None], cotangent, jnp.zeros((), BF16))
    keys_here = passage_keys[0]
    values_here = passage_values[0]
    key_count, width = keys_here.shape
    heads = width // DH
    positions = jnp.arange(key_count)
    owner = positions // PLEN
    passage_ids = jnp.arange(key_len.shape[1])
    key_lengths = jnp.sum(
        jnp.where(owner[:, None] == passage_ids[None, :], key_len[0][None, :], 0), axis=1
    )
    key_valid = positions % PLEN < key_lengths
    query_heads = queries.reshape(target_rows, heads, DH)
    key_heads = keys_here.reshape(key_count, heads, DH)
    value_heads = values_here.reshape(key_count, heads, DH)
    cot_heads = cotangent.reshape(target_rows, heads, DH)
    scores = (
        jnp.einsum("the,khe->htk", query_heads, key_heads, preferred_element_type=F32)
        * score_scale
    )
    scores = jnp.where(key_valid[None, None, :], scores, -jnp.inf)
    dprob = jnp.einsum("the,khe->htk", cot_heads, value_heads, preferred_element_type=F32)
    local_peak = jnp.max(scores, axis=2)
    local_expo = jnp.exp(scores - local_peak[:, :, None])
    peak, total, weighted = merged(
        (local_peak, jnp.sum(local_expo, axis=2), jnp.sum(local_expo * dprob, axis=2)),
        "passage",
        combine_stats,
    )
    expo = local_expo * jnp.exp(local_peak - peak)[:, :, None]
    probs = expo / total[:, :, None]
    row_dot = weighted / total
    probs_low = probs.astype(BF16)
    dscore = (probs * (dprob - row_dot[:, :, None])).astype(BF16)
    grad_values = jnp.einsum("htk,the->khe", probs_low, cot_heads, preferred_element_type=F32)
    grad_values = grad_values.reshape(key_count, width).astype(BF16)
    grad_keys = (
        jnp.einsum("htk,the->khe", dscore, query_heads, preferred_element_type=F32) * score_scale
    )
    grad_keys = grad_keys.reshape(key_count, width).astype(BF16)
    query_grad_part = (
        jnp.einsum("htk,khe->the", dscore, key_heads, preferred_element_type=F32) * score_scale
    )
    query_grad_part = query_grad_part.reshape(target_rows, width)
    query_grad = lax.psum(query_grad_part, "passage").astype(BF16)
    grad_states = lax.dot_general(query_grad, w_query, NT, preferred_element_type=F32)
    grad_states = grad_states.astype(BF16)
    weight_term = lax.dot_general(
        states, query_grad, (((0,), (0,)), ((), ())), preferred_element_type=F32
    )
    weight_term = weight_term / lax.axis_size("group")
    grad_query_weight = lax.psum_scatter(weight_term, "group", scatter_dimension=1, tiled=True)
    return (grad_states[None], grad_query_weight, grad_keys[None], grad_values[None])


def column(who, r, other):
    node, core = who[0] // 2, who[0] % 2
    return 2 * (node ^ r) + (1 - core if other else core)


def columns(who, r, other, width, start=0, size=None):
    offset = pl.multiple_of(column(who, r, other) * width + start, LANES)
    return pl.ds(offset, width if size is None else size)


SMEM_SPEC = pl.BlockSpec(memory_space=pltpu.SMEM)
VMEM_SPEC = pl.BlockSpec(memory_space=pltpu.VMEM)
ANY_SPEC = pl.BlockSpec(memory_space=pl.ANY)


def call(kernel, scalars, arrays, outs, aliases=None, far=(), out_specs=None, scratch=()):
    near = [pltpu.with_memory_space_constraint(x, pltpu.VMEM) for x in arrays]
    return pl.pallas_call(
        kernel,
        out_shape=outs,
        in_specs=[SMEM_SPEC] * len(scalars) + [VMEM_SPEC] * len(near) + [ANY_SPEC] * len(far),
        out_specs=[VMEM_SPEC] * len(outs) if out_specs is None else out_specs,
        input_output_aliases=aliases or {},
        scratch_shapes=scratch,
        compiler_params=pltpu.CompilerParams(vmem_limit_bytes=24 << 20),
    )(*scalars, *near, *far)


def vmem(shape, dtype):
    return pltpu.VMEM(shape, dtype)


def pack_call(who, keys, values, blocks, width):
    rows = keys.shape[0]

    def kernel(who_ref, k_ref, v_ref, o_ref, sem):
        copies = []
        for i, ref in enumerate((k_ref, v_ref)):
            for r in range(blocks):
                source = ref.at[:, columns(who_ref, r, True, width)]
                copies.append(pltpu.make_async_copy(source, o_ref.at[i, r], sem.at[i, r]))
        for copy in copies:
            copy.start()
        for copy in copies:
            copy.wait()

    return call(
        kernel,
        [who],
        [],
        [vmem((2, blocks, rows, width), BF16)],
        far=[keys, values],
        scratch=[pltpu.SemaphoreType.DMA((2, blocks))],
    )[0]


def project_call(who, states, weights, picks, width, addends=None):
    rows = states.shape[0]
    other = addends is None

    def kernel(who_ref, s_ref, w_ref, *rest):
        for i, r in enumerate(picks):
            block = w_ref[:, columns(who_ref, r, other, width)]
            part = jnp.dot(s_ref[...], block, preferred_element_type=F32)
            if other:
                rest[i][...] = part
            else:
                rest[len(picks) + i][...] = part + rest[i][...]

    return call(
        kernel, [who], [states, weights, *(addends or [])], [vmem((rows, width), F32)] * len(picks)
    )


def lane_half(shape, e):
    return lax.broadcasted_iota(jnp.int32, shape, 1) // DH == e


def key_bias(lens_ref, rows):
    slot = lax.broadcasted_iota(jnp.int32, (rows, 1), 0)
    limit = jnp.zeros((rows, 1), jnp.int32)
    for i in range(rows // PLEN):
        limit = jnp.where(slot // PLEN == i, lens_ref[i], limit)
    return jnp.where(slot % PLEN < limit, 0.0, -jnp.inf).astype(F32)


def masked_cot(tgt_ref, cot):
    row = lax.broadcasted_iota(jnp.int32, cot.shape, 0)
    return jnp.where(row < tgt_ref[0], cot, jnp.zeros((), cot.dtype))


SEGS = 2


def pair_of(who_ref, tgt_ref, refs, r, pair, width):
    q_ref, c_ref, k_ref, v_ref, m_ref = refs
    lanes = pl.ds(pair * LANES, LANES)
    own = columns(who_ref, r, False, width, pair * LANES, LANES)
    k = (k_ref[:, own], m_ref[0, r, :, lanes])
    v = (v_ref[:, own], m_ref[1, r, :, lanes])
    qs = q_ref[:, lanes] * jnp.asarray(DH ** (-0.5), BF16)
    return qs, masked_cot(tgt_ref, c_ref[:, lanes]), k, v


def stats_call(scalars, q, cot, keys, values, from_mate, r, stats):
    rows, width = q.shape
    slots = keys.shape[0]
    heads = width // DH
    blocks = from_mate.shape[1]

    def kernel(who_ref, len_ref, mate_ref, tgt_ref, *rest):
        o_ref = rest[-1]
        bias = (key_bias(len_ref, slots), key_bias(mate_ref, slots))
        for pair in range(width // LANES):
            qs, ct, k, v = pair_of(who_ref, tgt_ref, rest[:5], r, pair, width)
            for e in range(HPAIR):
                lanes = lane_half((rows, LANES), e)
                qm = jnp.where(lanes, qs, jnp.zeros((), BF16))
                cm = jnp.where(lanes, ct, jnp.zeros((), BF16))
                s = [lax.dot_general(k[i], qm, NT, preferred_element_type=F32) + bias[i] for i in range(SEGS)]
                d = [lax.dot_general(v[i], cm, NT, preferred_element_type=F32) for i in range(SEGS)]
                peak = jnp.maximum(*[jnp.max(x, axis=0, keepdims=True) for x in s])
                x = [jnp.exp(y - peak) for y in s]
                total = sum(jnp.sum(y, axis=0, keepdims=True) for y in x)
                weighted = sum(jnp.sum(y * w, axis=0, keepdims=True) for y, w in zip(x, d, strict=True))
                for kind, value in enumerate((peak, total, weighted)):
                    row = kind * heads + pair * HPAIR + e
                    o_ref[r, row : row + 1, :] = value

    arrays = [q, cot, keys, values, from_mate]
    aliases = None
    if stats is not None:
        aliases = {len(scalars) + len(arrays): 0}
        arrays.append(stats)
    return call(kernel, scalars, arrays, [vmem((blocks, 3 * heads, rows), F32)], aliases)[0]


def combined(mine, other, heads):
    peak = jnp.maximum(mine[:heads], other[:heads])
    mine_by, other_by = jnp.exp(mine[:heads] - peak), jnp.exp(other[:heads] - peak)
    total = mine[heads : 2 * heads] * mine_by + other[heads : 2 * heads] * other_by
    weighted = mine[2 * heads :] * mine_by + other[2 * heads :] * other_by
    return peak, total, weighted


def combine_call(stats, other, bit):
    blocks, kinds, _ = stats.shape
    heads = kinds // 3

    def kernel(s_ref, t_ref, o_ref):
        for r in range(blocks):
            for kind, x in enumerate(combined(s_ref[r], t_ref[r ^ bit], heads)):
                o_ref[r, kind * heads : (kind + 1) * heads, :] = x

    return call(kernel, [], [stats, other], [vmem(stats.shape, F32)])[0]


def grads_call(scalars, q, cot, keys, values, from_mate, stats, other, r, chain, out_type):
    rows, width = q.shape
    slots = keys.shape[0]
    heads = width // DH
    blocks = from_mate.shape[1]
    scale = DH ** (-0.5)
    bit = blocks // 2

    def kernel(who_ref, len_ref, mate_ref, tgt_ref, *rest):
        g_ref, o_ref, m_ref = rest[-3:]
        bias = (key_bias(len_ref, slots), key_bias(mate_ref, slots))
        peaks, totals, weights = combined(rest[5][r], rest[6][r ^ bit], heads)
        shares = 1.0 / totals
        dots = weights / totals
        for pair in range(width // LANES):
            qs, ct, k, v = pair_of(who_ref, tgt_ref, rest[:5], r, pair, width)
            grad_k = [None] * SEGS
            grad_v = [None] * SEGS
            grad_q = []
            turned = [x.T for x in k]
            for e in range(HPAIR):
                lanes = lane_half((rows, LANES), e)
                qm = jnp.where(lanes, qs, jnp.zeros((), BF16))
                cm = jnp.where(lanes, ct, jnp.zeros((), BF16))
                h = pair * HPAIR + e
                peak, share, dot = peaks[h : h + 1], shares[h : h + 1], dots[h : h + 1]
                part = 0.0
                for i in range(SEGS):
                    s = lax.dot_general(k[i], qm, NT, preferred_element_type=F32) + bias[i]
                    d = lax.dot_general(v[i], cm, NT, preferred_element_type=F32)
                    probs = jnp.exp(s - peak) * share
                    low = probs.astype(BF16)
                    ds = (probs * (d - dot)).astype(BF16)
                    gv = jnp.dot(low, cm, preferred_element_type=F32)
                    gk = jnp.dot(ds, qm, preferred_element_type=F32)
                    grad_v[i] = gv if e == 0 else grad_v[i] + gv
                    grad_k[i] = gk if e == 0 else grad_k[i] + gk
                    part = part + jnp.dot(
                        turned[i][e * DH : (e + 1) * DH], ds, preferred_element_type=F32
                    )
                grad_q.append(part)
            lanes = pl.ds(pair * LANES, LANES)
            g_ref[:, lanes] = (jnp.concatenate(grad_q, axis=0) * scale).T.astype(out_type)
            for i, ref in enumerate((o_ref, m_ref)):
                ref[0, r, :, lanes] = grad_k[i].astype(BF16)
                ref[1, r, :, lanes] = grad_v[i].astype(BF16)

    arrays = [q, cot, keys, values, from_mate, stats, other]
    aliases = None
    if chain is not None:
        aliases = {len(scalars) + len(arrays) + i: 1 + i for i in range(2)}
        arrays += chain
    stack = vmem((2, blocks, slots, width), BF16)
    out = call(kernel, scalars, arrays, [vmem((rows, width), out_type), stack, stack], aliases)
    return out[0], list(out[1:])


def place_call(who, own, from_mate, full):
    _, blocks, slots, width = own.shape

    def kernel(who_ref, o_ref, m_ref, k_ref, v_ref, sem):
        copies = []
        for i, target in enumerate((k_ref, v_ref)):
            for j, source in enumerate((o_ref, m_ref)):
                for r in range(blocks):
                    there = target.at[:, columns(who_ref, r, j == 1, width)]
                    copies.append(pltpu.make_async_copy(source.at[i, r], there, sem.at[i, j, r]))
        for copy in copies:
            copy.start()
        for copy in copies:
            copy.wait()

    return call(
        kernel,
        [who],
        [own, from_mate],
        [jax.ShapeDtypeStruct((slots, full), BF16)] * 2,
        out_specs=[ANY_SPEC] * 2,
        scratch=[pltpu.SemaphoreType.DMA((2, 2, blocks))],
    )


def states_call(who, mine, mates, weights):
    blocks = len(mine)
    rows, width = mine[0].shape
    depth = weights.shape[0]

    def kernel(who_ref, *rest):
        w_ref, o_ref = rest[-2:]
        total = 0.0
        for j in range(2):
            for r in range(blocks):
                block = w_ref[:, columns(who_ref, r, j == 1, width)]
                total += lax.dot_general(
                    rest[j * blocks + r][...], block, NT, preferred_element_type=F32
                )
        o_ref[...] = total.astype(BF16)

    return call(
        kernel, [who], [*mine, *mates, weights], [jax.ShapeDtypeStruct((rows, depth), BF16)]
    )[0]


def route_call(who, mine, groups):
    rows, width = mine[0].shape

    def kernel(who_ref, *rest):
        node, group = who_ref[0] // 2, who_ref[1]
        for s in range(groups):
            for r in range(len(mine)):

                @pl.when((group ^ s) ^ node == r)
                def _(s=s, r=r):
                    rest[len(mine) + s][...] = rest[r][...]

    return call(kernel, [who], mine, [vmem((rows, width), BF16)] * groups)


def turn_call(questions):
    rows, depth = questions[0].shape

    def kernel(*refs):
        for s, ref in enumerate(refs[:-1]):
            refs[-1][:, s * rows : (s + 1) * rows] = ref[...].T

    return call(kernel, [], questions, [vmem((depth, rows * len(questions)), BF16)])[0]


def weight_call(who, turned, blocks, other, half):
    depth = turned.shape[0]
    groups = len(blocks)
    rows, width = blocks[0].shape

    def kernel(who_ref, s_ref, *rest):
        held, sem = rest[-2:]
        target = rest[-3]
        total = 0.0
        for s in range(groups):
            total += jnp.dot(
                s_ref[:, s * rows : (s + 1) * rows], rest[s][...], preferred_element_type=F32
            )
        held[...] = total / groups
        core = who_ref[0] % 2
        side = 1 - core if other else core
        there = target.at[:, pl.ds(pl.multiple_of(side * width, LANES), width)]
        copy = pltpu.make_async_copy(held, there, sem)
        copy.start()
        copy.wait()

    return call(
        kernel,
        [who],
        [turned, *blocks],
        [jax.ShapeDtypeStruct((depth, 2 * width), F32)],
        aliases=None if half is None else {2 + groups: 0},
        far=[] if half is None else [half],
        out_specs=[ANY_SPEC],
        scratch=[pltpu.VMEM((depth, width), F32), pltpu.SemaphoreType.DMA],
    )[0]


def swap(x, bit):
    count = lax.axis_size("passage")
    return lax.ppermute(x, "passage", [(i, i ^ bit) for i in range(count)])


def group_swap(x, bits):
    count = lax.axis_size("group")
    return lax.ppermute(x, "group", [(i, i ^ bits) for i in range(count)])


def halve(pieces, nodes, wire=F32):
    bit = 1
    while bit < nodes:
        sent = [r for r in range(nodes - 1, -1, -1) if r & bit and r % bit == 0]
        for r in sent:
            got = swap(pieces[r].astype(wire), 2 * bit)
            pieces[r ^ bit] = pieces[r ^ bit] + got.astype(F32)
        bit *= 2
    return pieces[0]


def double(own, nodes):
    held = {0: own}
    bit = nodes // 2
    while bit:
        held.update({r ^ bit: swap(x, 2 * bit) for r, x in list(held.items())})
        bit //= 2
    return [held[r] for r in range(nodes)]


def on_device(
    decoder_states, w_query, passage_keys, passage_values, grad_context, key_len, tgt_len
):
    return on_device_inner(
        decoder_states, w_query, passage_keys, passage_values, grad_context, key_len, tgt_len
    )


def on_device_inner(
    decoder_states, w_query, passage_keys, passage_values, grad_context, key_len, tgt_len
):
    nodes = lax.axis_size("passage") // 2
    groups = lax.axis_size("group")
    me, group = lax.axis_index("passage"), lax.axis_index("group")
    who = jnp.where(jnp.arange(2) == 0, me, group).astype(jnp.int32)
    states = decoder_states[0]
    keys, values = passage_keys[0], passage_values[0]
    width = grad_context.shape[2]

    cots = double(grad_context[0], nodes)
    odd = list(range(nodes - 1, -1, -2))
    even = list(range(nodes - 2, -1, -2))
    parts = {}
    mates = {}
    for picks in (odd, even):
        for r, x in zip(picks, project_call(who, states, w_query, picks, width), strict=True):
            mates[r] = swap(x, 1)
    for picks in (odd, even):
        out = project_call(who, states, w_query, picks, width, [mates[r] for r in picks])
        parts.update(zip(picks, out, strict=True))
    own_query = halve(parts, nodes).astype(BF16)
    queries = double(own_query, nodes)

    mate_len = swap(key_len[0], 1)
    from_mate = swap(pack_call(who, keys, values, nodes, width), 1)
    scalars = (who, key_len[0], mate_len, tgt_len)
    questions = [states] + [group_swap(states, s) for s in range(1, groups)]
    turned = turn_call(questions)

    stats = None
    for r in sorted(range(nodes), key=lambda r: (r & 1, r)):
        stats = stats_call(scalars, queries[r], cots[r], keys, values, from_mate, r, stats)
    bit = 1
    while bit < nodes // 2:
        stats = combine_call(stats, swap(stats, 2 * bit), bit)
        bit *= 2
    other = swap(stats, 2 * bit)

    parts, chain = {}, None
    for r in range(nodes - 1, -1, -1):
        out_type = BF16 if r & 1 else F32
        parts[r], chain = grads_call(
            scalars, queries[r], cots[r], keys, values, from_mate, stats, other, r, chain, out_type
        )
    own_grad = halve(parts, nodes, BF16).astype(BF16)
    grad_k, grad_v = place_call(who, chain[0], swap(chain[1], 1), keys.shape[1])
    mine = double(own_grad, nodes)
    routed = route_call(who, mine, groups)
    got = [routed[0]] + [group_swap(routed[s], s) for s in range(1, groups)]
    weight = weight_call(who, turned, got, False, None)
    weight = weight_call(who, turned, [swap(x, 1) for x in got], True, weight)
    beside = [swap(x, 1) for x in mine]
    grad_states = states_call(who, mine, beside, w_query)
    return (grad_states[None], weight, grad_k[None], grad_v[None])


def solution(mesh):
    placed = (
        P("group", None, "passage"),
        P("passage", None),
        P("group", "passage", None),
        P("group", "passage", None),
        P("group", None, "passage"),
        P("group", "passage"),
        P("group"),
    )

    def whole(*args):
        groups, count = mesh.shape["group"], mesh.shape["passage"]
        paired = 2 * groups == count and count & (count - 1) == 0
        blocked = args[4].shape[2] % (count * LANES) == 0
        body = on_device if paired and blocked else on_device_general
        return jax.shard_map(
            body,
            mesh=mesh,
            in_specs=placed,
            out_specs=(
                P("group", None, "passage"),
                P("passage", "group"),
                P("group", "passage", None),
                P("group", "passage", None),
            ),
            check_vma=False,
        )(*args)

    return whole
```

```python
import functools

import jax
import jax.numpy as jnp
from jax import lax
from jax.experimental import pallas as pl
from jax.experimental.pallas import tpu as pltpu
from jax.sharding import PartitionSpec as P


DH = 64
PLEN = 128
LANES = 128
HPAIR = LANES // DH
F32 = jnp.float32
BF16 = jnp.bfloat16
NT = (((1,), (1,)), ((), ()))


def merged(part, axis, combine):
    gathered = jax.tree.map(lambda a: lax.all_gather(a, axis), part)

    def take(source):
        return jax.tree.map(lambda a: lax.dynamic_index_in_dim(a, source, 0, False), gathered)

    return lax.fori_loop(
        1, lax.axis_size(axis), lambda source, state: combine(state, take(source)), take(0)
    )


def combine_stats(earlier, later):
    peak_a, total_a, weighted_a = earlier
    peak_b, total_b, weighted_b = later
    peak = jnp.maximum(peak_a, peak_b)
    factor_a = jnp.exp(peak_a - peak)
    factor_b = jnp.exp(peak_b - peak)
    return (
        peak,
        total_a * factor_a + total_b * factor_b,
        weighted_a * factor_a + weighted_b * factor_b,
    )


def on_device_general(
    decoder_states, w_query, passage_keys, passage_values, grad_context, key_len, tgt_len
):
    score_scale = DH ** (-0.5)
    states = decoder_states[0]
    target_rows = states.shape[0]
    query_part = jnp.dot(states, w_query, preferred_element_type=F32)
    queries = lax.psum(query_part, "passage").astype(BF16)
    cotangent = lax.all_gather(grad_context[0], "passage", axis=1, tiled=True)
    row_valid = jnp.arange(target_rows) < tgt_len[0]
    cotangent = jnp.where(row_valid[:, None], cotangent, jnp.zeros((), BF16))
    keys_here = passage_keys[0]
    values_here = passage_values[0]
    key_count, width = keys_here.shape
    heads = width // DH
    positions = jnp.arange(key_count)
    owner = positions // PLEN
    passage_ids = jnp.arange(key_len.shape[1])
    key_lengths = jnp.sum(
        jnp.where(owner[:, None] == passage_ids[None, :], key_len[0][None, :], 0), axis=1
    )
    key_valid = positions % PLEN < key_lengths
    query_heads = queries.reshape(target_rows, heads, DH)
    key_heads = keys_here.reshape(key_count, heads, DH)
    value_heads = values_here.reshape(key_count, heads, DH)
    cot_heads = cotangent.reshape(target_rows, heads, DH)
    scores = (
        jnp.einsum("the,khe->htk", query_heads, key_heads, preferred_element_type=F32)
        * score_scale
    )
    scores = jnp.where(key_valid[None, None, :], scores, -jnp.inf)
    dprob = jnp.einsum("the,khe->htk", cot_heads, value_heads, preferred_element_type=F32)
    local_peak = jnp.max(scores, axis=2)
    local_expo = jnp.exp(scores - local_peak[:, :, None])
    peak, total, weighted = merged(
        (local_peak, jnp.sum(local_expo, axis=2), jnp.sum(local_expo * dprob, axis=2)),
        "passage",
        combine_stats,
    )
    expo = local_expo * jnp.exp(local_peak - peak)[:, :, None]
    probs = expo / total[:, :, None]
    row_dot = weighted / total
    probs_low = probs.astype(BF16)
    dscore = (probs * (dprob - row_dot[:, :, None])).astype(BF16)
    grad_values = jnp.einsum("htk,the->khe", probs_low, cot_heads, preferred_element_type=F32)
    grad_values = grad_values.reshape(key_count, width).astype(BF16)
    grad_keys = (
        jnp.einsum("htk,the->khe", dscore, query_heads, preferred_element_type=F32) * score_scale
    )
    grad_keys = grad_keys.reshape(key_count, width).astype(BF16)
    query_grad_part = (
        jnp.einsum("htk,khe->the", dscore, key_heads, preferred_element_type=F32) * score_scale
    )
    query_grad_part = query_grad_part.reshape(target_rows, width)
    query_grad = lax.psum(query_grad_part, "passage").astype(BF16)
    grad_states = lax.dot_general(query_grad, w_query, NT, preferred_element_type=F32)
    grad_states = grad_states.astype(BF16)
    weight_term = lax.dot_general(
        states, query_grad, (((0,), (0,)), ((), ())), preferred_element_type=F32
    )
    weight_term = weight_term / lax.axis_size("group")
    grad_query_weight = lax.psum_scatter(weight_term, "group", scatter_dimension=1, tiled=True)
    return (grad_states[None], grad_query_weight, grad_keys[None], grad_values[None])


def column(who, r, other):
    node, core = who[0] // 2, who[0] % 2
    return 2 * (node ^ r) + (1 - core if other else core)


def columns(who, r, other, width, start=0, size=None):
    offset = pl.multiple_of(column(who, r, other) * width + start, LANES)
    return pl.ds(offset, width if size is None else size)


SMEM_SPEC = pl.BlockSpec(memory_space=pltpu.SMEM)
VMEM_SPEC = pl.BlockSpec(memory_space=pltpu.VMEM)
ANY_SPEC = pl.BlockSpec(memory_space=pl.ANY)


def call(kernel, scalars, arrays, outs, aliases=None, far=(), out_specs=None, scratch=()):
    near = [pltpu.with_memory_space_constraint(x, pltpu.VMEM) for x in arrays]
    return pl.pallas_call(
        kernel,
        out_shape=outs,
        in_specs=[SMEM_SPEC] * len(scalars) + [VMEM_SPEC] * len(near) + [ANY_SPEC] * len(far),
        out_specs=[VMEM_SPEC] * len(outs) if out_specs is None else out_specs,
        input_output_aliases=aliases or {},
        scratch_shapes=scratch,
        compiler_params=pltpu.CompilerParams(vmem_limit_bytes=24 << 20),
    )(*scalars, *near, *far)


def vmem(shape, dtype):
    return pltpu.VMEM(shape, dtype)


def pack_call(who, keys, values, blocks, width):
    rows = keys.shape[0]

    def kernel(who_ref, k_ref, v_ref, o_ref, sem):
        copies = []
        for i, ref in enumerate((k_ref, v_ref)):
            for r in range(blocks):
                source = ref.at[:, columns(who_ref, r, True, width)]
                copies.append(pltpu.make_async_copy(source, o_ref.at[i, r], sem.at[i, r]))
        for copy in copies:
            copy.start()
        for copy in copies:
            copy.wait()

    return call(
        kernel,
        [who],
        [],
        [vmem((2, blocks, rows, width), BF16)],
        far=[keys, values],
        scratch=[pltpu.SemaphoreType.DMA((2, blocks))],
    )[0]


def project_call(who, states, weights, picks, width, addends=None):
    rows = states.shape[0]
    other = addends is None

    def kernel(who_ref, s_ref, w_ref, *rest):
        for i, r in enumerate(picks):
            block = w_ref[:, columns(who_ref, r, other, width)]
            part = jnp.dot(s_ref[...], block, preferred_element_type=F32)
            if other:
                rest[i][...] = part
            else:
                rest[len(picks) + i][...] = part + rest[i][...]

    return call(
        kernel, [who], [states, weights, *(addends or [])], [vmem((rows, width), F32)] * len(picks)
    )


def lane_half(shape, e):
    return lax.broadcasted_iota(jnp.int32, shape, 1) // DH == e


def key_bias(lens_ref, rows):
    slot = lax.broadcasted_iota(jnp.int32, (rows, 1), 0)
    limit = jnp.zeros((rows, 1), jnp.int32)
    for i in range(rows // PLEN):
        limit = jnp.where(slot // PLEN == i, lens_ref[i], limit)
    return jnp.where(slot % PLEN < limit, 0.0, -jnp.inf).astype(F32)


def masked_cot(tgt_ref, cot):
    row = lax.broadcasted_iota(jnp.int32, cot.shape, 0)
    return jnp.where(row < tgt_ref[0], cot, jnp.zeros((), cot.dtype))


SEGS = 2


def pair_of(who_ref, tgt_ref, refs, r, pair, width):
    q_ref, c_ref, k_ref, v_ref, m_ref = refs
    lanes = pl.ds(pair * LANES, LANES)
    own = columns(who_ref, r, False, width, pair * LANES, LANES)
    k = (k_ref[:, own], m_ref[0, r, :, lanes])
    v = (v_ref[:, own], m_ref[1, r, :, lanes])
    qs = q_ref[:, lanes] * jnp.asarray(DH ** (-0.5), BF16)
    return qs, masked_cot(tgt_ref, c_ref[:, lanes]), k, v


def stats_call(scalars, q, cot, keys, values, from_mate, r, stats):
    rows, width = q.shape
    slots = keys.shape[0]
    heads = width // DH
    blocks = from_mate.shape[1]

    def kernel(who_ref, len_ref, mate_ref, tgt_ref, *rest):
        o_ref = rest[-1]
        bias = (key_bias(len_ref, slots), key_bias(mate_ref, slots))
        for pair in range(width // LANES):
            qs, ct, k, v = pair_of(who_ref, tgt_ref, rest[:5], r, pair, width)
            for e in range(HPAIR):
                lanes = lane_half((rows, LANES), e)
                qm = jnp.where(lanes, qs, jnp.zeros((), BF16))
                cm = jnp.where(lanes, ct, jnp.zeros((), BF16))
                s = [lax.dot_general(k[i], qm, NT, preferred_element_type=F32) + bias[i] for i in range(SEGS)]
                d = [lax.dot_general(v[i], cm, NT, preferred_element_type=F32) for i in range(SEGS)]
                peak = jnp.maximum(*[jnp.max(x, axis=0, keepdims=True) for x in s])
                x = [jnp.exp(y - peak) for y in s]
                total = sum(jnp.sum(y, axis=0, keepdims=True) for y in x)
                weighted = sum(jnp.sum(y * w, axis=0, keepdims=True) for y, w in zip(x, d, strict=True))
                for kind, value in enumerate((peak + jnp.log(total), weighted / total)):
                    row = kind * heads + pair * HPAIR + e
                    o_ref[r, row : row + 1, :] = value

    arrays = [q, cot, keys, values, from_mate]
    aliases = None
    if stats is not None:
        aliases = {len(scalars) + len(arrays): 0}
        arrays.append(stats)
    return call(kernel, scalars, arrays, [vmem((blocks, 2 * heads, rows), F32)], aliases)[0]


def grads_call(scalars, q, cot, keys, values, from_mate, stats, r, chain, out_type):
    rows, width = q.shape
    slots = keys.shape[0]
    heads = width // DH
    blocks = from_mate.shape[1]
    scale = DH ** (-0.5)

    def kernel(who_ref, len_ref, mate_ref, tgt_ref, *rest):
        g_ref, o_ref, m_ref = rest[-3:]
        bias = (key_bias(len_ref, slots), key_bias(mate_ref, slots))
        held = [rest[5 + i][r ^ i] for i in range(blocks)]
        peaks = functools.reduce(jnp.maximum, [x[:heads] for x in held])
        factors = [jnp.exp(x[:heads] - peaks) for x in held]
        shares = 1.0 / sum(factors)
        dots = shares * sum(f * x[heads:] for f, x in zip(factors, held, strict=True))
        for pair in range(width // LANES):
            qs, ct, k, v = pair_of(who_ref, tgt_ref, rest[:5], r, pair, width)
            grad_k = [None] * SEGS
            grad_v = [None] * SEGS
            grad_q = []
            turned = [x.T for x in k]
            for e in range(HPAIR):
                lanes = lane_half((rows, LANES), e)
                qm = jnp.where(lanes, qs, jnp.zeros((), BF16))
                cm = jnp.where(lanes, ct, jnp.zeros((), BF16))
                h = pair * HPAIR + e
                peak, share, dot = peaks[h : h + 1], shares[h : h + 1], dots[h : h + 1]
                part = 0.0
                for i in range(SEGS):
                    s = lax.dot_general(k[i], qm, NT, preferred_element_type=F32) + bias[i]
                    d = lax.dot_general(v[i], cm, NT, preferred_element_type=F32)
                    probs = jnp.exp(s - peak) * share
                    low = probs.astype(BF16)
                    ds = (probs * (d - dot)).astype(BF16)
                    gv = jnp.dot(low, cm, preferred_element_type=F32)
                    gk = jnp.dot(ds, qm, preferred_element_type=F32)
                    grad_v[i] = gv if e == 0 else grad_v[i] + gv
                    grad_k[i] = gk if e == 0 else grad_k[i] + gk
                    part = part + jnp.dot(
                        turned[i][e * DH : (e + 1) * DH], ds, preferred_element_type=F32
                    )
                grad_q.append(part)
            lanes = pl.ds(pair * LANES, LANES)
            g_ref[:, lanes] = (jnp.concatenate(grad_q, axis=0) * scale).T.astype(out_type)
            for i, ref in enumerate((o_ref, m_ref)):
                ref[0, r, :, lanes] = grad_k[i].astype(BF16)
                ref[1, r, :, lanes] = grad_v[i].astype(BF16)

    arrays = [q, cot, keys, values, from_mate, *stats]
    aliases = None
    if chain is not None:
        aliases = {len(scalars) + len(arrays) + i: 1 + i for i in range(2)}
        arrays += chain
    stack = vmem((2, blocks, slots, width), BF16)
    out = call(kernel, scalars, arrays, [vmem((rows, width), out_type), stack, stack], aliases)
    return out[0], list(out[1:])


def place_call(who, own, from_mate, full):
    _, blocks, slots, width = own.shape

    def kernel(who_ref, o_ref, m_ref, k_ref, v_ref, sem):
        copies = []
        for i, target in enumerate((k_ref, v_ref)):
            for j, source in enumerate((o_ref, m_ref)):
                for r in range(blocks):
                    there = target.at[:, columns(who_ref, r, j == 1, width)]
                    copies.append(pltpu.make_async_copy(source.at[i, r], there, sem.at[i, j, r]))
        for copy in copies:
            copy.start()
        for copy in copies:
            copy.wait()

    return call(
        kernel,
        [who],
        [own, from_mate],
        [jax.ShapeDtypeStruct((slots, full), BF16)] * 2,
        out_specs=[ANY_SPEC] * 2,
        scratch=[pltpu.SemaphoreType.DMA((2, 2, blocks))],
    )


def states_call(who, mine, mates, weights):
    blocks = len(mine)
    rows, width = mine[0].shape
    depth = weights.shape[0]

    def kernel(who_ref, *rest):
        w_ref, o_ref = rest[-2:]
        total = 0.0
        for j in range(2):
            for r in range(blocks):
                block = w_ref[:, columns(who_ref, r, j == 1, width)]
                total += lax.dot_general(
                    rest[j * blocks + r][...], block, NT, preferred_element_type=F32
                )
        o_ref[...] = total.astype(BF16)

    return call(
        kernel, [who], [*mine, *mates, weights], [jax.ShapeDtypeStruct((rows, depth), BF16)]
    )[0]


def route_call(who, mine, groups):
    rows, width = mine[0].shape

    def kernel(who_ref, *rest):
        node, group = who_ref[0] // 2, who_ref[1]
        for s in range(groups):
            for r in range(len(mine)):

                @pl.when((group ^ s) ^ node == r)
                def _(s=s, r=r):
                    rest[len(mine) + s][...] = rest[r][...]

    return call(kernel, [who], mine, [vmem((rows, width), BF16)] * groups)


def turn_call(questions):
    rows, depth = questions[0].shape

    def kernel(*refs):
        for s, ref in enumerate(refs[:-1]):
            refs[-1][:, s * rows : (s + 1) * rows] = ref[...].T

    return call(kernel, [], questions, [vmem((depth, rows * len(questions)), BF16)])[0]


def weight_call(who, turned, blocks, other, half):
    depth = turned.shape[0]
    groups = len(blocks)
    rows, width = blocks[0].shape

    def kernel(who_ref, s_ref, *rest):
        held, sem = rest[-2:]
        target = rest[-3]
        total = 0.0
        for s in range(groups):
            total += jnp.dot(
                s_ref[:, s * rows : (s + 1) * rows], rest[s][...], preferred_element_type=F32
            )
        held[...] = total / groups
        core = who_ref[0] % 2
        side = 1 - core if other else core
        there = target.at[:, pl.ds(pl.multiple_of(side * width, LANES), width)]
        copy = pltpu.make_async_copy(held, there, sem)
        copy.start()
        copy.wait()

    return call(
        kernel,
        [who],
        [turned, *blocks],
        [jax.ShapeDtypeStruct((depth, 2 * width), F32)],
        aliases=None if half is None else {2 + groups: 0},
        far=[] if half is None else [half],
        out_specs=[ANY_SPEC],
        scratch=[pltpu.VMEM((depth, width), F32), pltpu.SemaphoreType.DMA],
    )[0]


def swap(x, bit):
    count = lax.axis_size("passage")
    return lax.ppermute(x, "passage", [(i, i ^ bit) for i in range(count)])


def group_swap(x, bits):
    count = lax.axis_size("group")
    return lax.ppermute(x, "group", [(i, i ^ bits) for i in range(count)])


def halve(pieces, nodes, wire=F32):
    bit = 1
    while bit < nodes:
        sent = [r for r in range(nodes - 1, -1, -1) if r & bit and r % bit == 0]
        for r in sent:
            got = swap(pieces[r].astype(wire), 2 * bit)
            pieces[r ^ bit] = pieces[r ^ bit] + got.astype(F32)
        bit *= 2
    return pieces[0]


def double(own, nodes):
    held = {0: own}
    bit = nodes // 2
    while bit:
        held.update({r ^ bit: swap(x, 2 * bit) for r, x in list(held.items())})
        bit //= 2
    return [held[r] for r in range(nodes)]


def on_device(
    decoder_states, w_query, passage_keys, passage_values, grad_context, key_len, tgt_len
):
    return on_device_inner(
        decoder_states, w_query, passage_keys, passage_values, grad_context, key_len, tgt_len
    )


def on_device_inner(
    decoder_states, w_query, passage_keys, passage_values, grad_context, key_len, tgt_len
):
    nodes = lax.axis_size("passage") // 2
    groups = lax.axis_size("group")
    me, group = lax.axis_index("passage"), lax.axis_index("group")
    who = jnp.where(jnp.arange(2) == 0, me, group).astype(jnp.int32)
    states = decoder_states[0]
    keys, values = passage_keys[0], passage_values[0]
    width = grad_context.shape[2]

    cots = double(grad_context[0], nodes)
    odd = list(range(nodes - 1, -1, -2))
    even = list(range(nodes - 2, -1, -2))
    parts = {}
    mates = {}
    for picks in (odd, even):
        out = project_call(who, states, w_query, picks, width)
        for r, x in zip(picks, out, strict=True):
            mates[r] = swap(x, 1)
    for picks in (odd, even):
        addends = [mates[r] for r in picks]
        out = project_call(who, states, w_query, picks, width, addends)
        parts.update(zip(picks, out, strict=True))
    own_query = halve(parts, nodes).astype(BF16)
    queries = double(own_query, nodes)

    mate_len = swap(key_len[0], 1)
    from_mate = swap(pack_call(who, keys, values, nodes, width), 1)
    scalars = (who, key_len[0], mate_len, tgt_len)
    questions = [states] + [group_swap(states, s) for s in range(1, groups)]
    turned = turn_call(questions)

    stats = None
    for r in STATS_ORDER if nodes == 4 else range(nodes):
        stats = stats_call(scalars, queries[r], cots[r], keys, values, from_mate, r, stats)
    stats = [stats] + [swap(stats, 2 * i) for i in range(1, nodes)]

    parts, chain = {}, None
    for r in range(nodes - 1, -1, -1):
        out_type = BF16 if r & 1 else F32
        args = (scalars, queries[r], cots[r], keys, values, from_mate, stats, r, chain, out_type)
        parts[r], chain = grads_call(*args)
    own_grad = halve(parts, nodes, BF16).astype(BF16)
    back = swap(chain[1], 1)
    grad_k, grad_v = place_call(who, chain[0], back, keys.shape[1])
    mine = double(own_grad, nodes)
    routed = route_call(who, mine, groups)
    got = [routed[0]] + [group_swap(routed[s], s) for s in range(1, groups)]
    weight = weight_call(who, turned, got, False, None)
    crossed = [swap(x, 1) for x in got]
    weight = weight_call(who, turned, crossed, True, weight)
    beside = [swap(x, 1) for x in mine]
    grad_states = states_call(who, mine, beside, w_query)
    return (grad_states[None], weight, grad_k[None], grad_v[None])


STATS_ORDER = (0, 1, 2, 3)


def solution(mesh):
    placed = (
        P("group", None, "passage"),
        P("passage", None),
        P("group", "passage", None),
        P("group", "passage", None),
        P("group", None, "passage"),
        P("group", "passage"),
        P("group"),
    )

    def whole(*args):
        groups, count = mesh.shape["group"], mesh.shape["passage"]
        paired = 2 * groups == count and count & (count - 1) == 0
        blocked = args[4].shape[2] % (count * LANES) == 0
        body = on_device if paired and blocked else on_device_general
        mapped = jax.shard_map(
            body,
            mesh=mesh,
            in_specs=placed,
            out_specs=(
                P("group", None, "passage"),
                P("passage", "group"),
                P("group", "passage", None),
                P("group", "passage", None),
            ),
            check_vma=False,
        )
        return mapped(*args)

    return whole
```
